32 devices in a mesh: fsdp: 8 (over z, core), ctx: 2 (over y), tp: 2 (over x).
Axes of the slice: x: 2, y: 2, z: 4, core: 2. Of those that a mesh axis runs over, the one named last changes fastest.
Arguments:
- inputs: bfloat16 [8, 2048, 1024], P('fsdp', 'ctx'), may hold values from -6 to 6
- cotangent: bfloat16 [8, 2048, 1024], P('fsdp', 'ctx'), may hold values from -6 to 6
- segment_ids: int32 [8, 2048], P('fsdp'), may hold values from 0 to 23, never falling along the last dimension, each value on 1 to 1024 neighbouring positions
- norm_gain: bfloat16 [1024], P(('fsdp', 'ctx')), may hold values from 0.5 to 1.5
- norm_shift: bfloat16 [1024], P(('fsdp', 'ctx')), may hold values from -3 to 3
- qkv_weight: bfloat16 [1024, 3072], P(('fsdp', 'ctx'), 'tp'), may hold values from -0.1875 to 0.1875
- qkv_bias: bfloat16 [96, 32], P('tp', ('fsdp', 'ctx')), may hold values from -3 to 3
- dense_weight: bfloat16 [1024, 1024], P('tp', ('fsdp', 'ctx')), may hold values from -0.75 to 0.75
- dense_bias: bfloat16 [1024], P(('fsdp', 'ctx')), may hold values from -3 to 3
- expand_weight: bfloat16 [1024, 4096], P(('fsdp', 'ctx'), 'tp'), may hold values from -0.1875 to 0.1875
- expand_bias: bfloat16 [128, 32], P('tp', ('fsdp', 'ctx')), may hold values from -3 to 3
- shrink_weight: bfloat16 [4096, 1024], P('tp', ('fsdp', 'ctx')), may hold values from -0.09375 to 0.09375
- shrink_bias: bfloat16 [1024], P(('fsdp', 'ctx')), may hold values from -3 to 3
Outputs:
- layer_output: bfloat16 [8, 2048, 1024], P('fsdp', 'ctx')
- input_grad: float32 [8, 2048, 1024], P('fsdp', 'ctx')
- norm_gain_grad: float32 [1024], P(('fsdp', 'ctx'))
- norm_shift_grad: float32 [1024], P(('fsdp', 'ctx'))
- qkv_weight_grad: float32 [1024, 3072], P(('fsdp', 'ctx'), 'tp')
- qkv_bias_grad: float32 [96, 32], P('tp', ('fsdp', 'ctx'))
- dense_weight_grad: float32 [1024, 1024], P('tp', ('fsdp', 'ctx'))
- dense_bias_grad: float32 [1024], P(('fsdp', 'ctx'))
- expand_weight_grad: float32 [1024, 4096], P(('fsdp', 'ctx'), 'tp')
- expand_bias_grad: float32 [128, 32], P('tp', ('fsdp', 'ctx'))
- shrink_weight_grad: float32 [4096, 1024], P('tp', ('fsdp', 'ctx'))
- shrink_bias_grad: float32 [1024], P(('fsdp', 'ctx'))
The draws below stay inside these ranges and needn't reach their ends.
Inputs may be any that keep to these rules, and one draw needn't show every extreme that they name: `segment_ids`: along each sequence the document numbers never fall; each of the 24 documents has 1 to 1024 tokens, and some document has exactly 1024.
All inputs are finite; a program needn't handle non-finite values.
Results may differ from the reference program's by a relative error of at most 0.009.
Values may be sent and summed in bfloat16 or wider, within the bound.
No kernel may reach another device: no remote copies, remote signals or barrier semaphores. Data moves between devices by JAX's collectives and lax.ppermute only.
A program may use at most 256 MiB of HBM per device.

```python
import math
from functools import partial
import jax
import jax.numpy as jnp
import numpy as np
from jax import lax

D = 1024
H = 16
FF = 4096
DH = 64
ROT = 16
LEN = 2048
SEQS = 8


def level_of(stream_key, extent, cuts, least, top_value):
    def one(position, blocks):
        draws = jax.random.uniform(jax.random.fold_in(jax.random.fold_in(stream_key, 6), position), (blocks,), jnp.float32, least / len(cuts), top_value / len(cuts))
        return jnp.repeat(jnp.exp(draws), extent[position] // blocks).reshape((-1,) + (1,) * (len(extent) - position - 1))

    gain = one(*cuts[0])
    for cut in cuts[1:]:
        gain = gain * one(*cut)
    return gain


def split_up(count, total, bound, slope):
    portions = [(1 << 20) // math.isqrt(rank ** slope) + 1 for rank in range(2, count + 1)]
    surplus, holding = total - bound - (count - 1), [1] * (count - 1)
    while surplus > 0:
        movable = [i for i in range(count - 1) if holding[i] < bound]
        pool, left = sum([portions[i] for i in movable]), surplus
        for i in movable:
            addition = min(bound - holding[i], max(1, left * portions[i] // pool), surplus)
            holding[i] = holding[i] + addition
            surplus = surplus - addition
    return np.array([bound] + holding)


def uneven_parts(rng, count, total, bound, lean):
    if count == 2:
        one = jax.random.randint(rng, (), max(1, total - bound), min(bound, total - 1) + 1)
        return jnp.stack([one, total - one])
    tallies = jnp.asarray(split_up(count, total, bound, lean), jnp.int32)
    couples = (count - 1) // 2
    source_of, receiver = tallies[1:1 + 2 * couples:2], tallies[2:2 + 2 * couples:2]
    margin = jnp.minimum(source_of - 1, bound - receiver)
    passed = jax.random.randint(jax.random.fold_in(rng, 1), (couples,), 0, 1 << 20) % (margin + 1)
    tallies = tallies.at[1:1 + 2 * couples:2].set(source_of - passed).at[2:2 + 2 * couples:2].set(receiver + passed)
    return tallies[jax.random.permutation(jax.random.fold_in(rng, 2), count)]


def noise(stream_key, dims, deviation, limit, shards=(), held_as=jnp.bfloat16):
    values = jax.random.normal(stream_key, dims, jnp.float32) * deviation
    if len(shards) > 0:
        values = level_of(stream_key, dims, shards, -0.22, 0.18) * values
    return jnp.clip(values, min=-limit, max=limit).astype(held_as)


def setup_inputs(seed: int = 0) -> dict:
    keys = jax.random.split(jax.random.key(seed), 14)
    inputs = noise(keys[0], (SEQS, LEN, D), 1.0, 6.0, ((0, 8), (1, 2)))
    cotangent = noise(keys[1], (SEQS, LEN, D), 1.0, 6.0, ((0, 8), (1, 2)))
    segment_ids = jax.vmap(lambda own: jnp.searchsorted(jnp.cumsum(uneven_parts(own, min(24, LEN // 4), LEN, LEN // 2, 2)), jnp.arange(LEN), side="right"))(jax.random.split(keys[2], SEQS)).reshape((SEQS, LEN)).astype(jnp.int32)
    norm_gain = jnp.clip(1.0 + 0.1 * jax.random.normal(keys[3], (D,), jnp.float32), 0.5, 1.5).astype(jnp.bfloat16)
    norm_shift = noise(keys[4], (D,), 0.5, 3.0, ((0, 16),))
    qkv_weight = noise(keys[5], (D, 3 * D), D ** -0.5, 0.1875, ((0, 16), (1, 2)))
    qkv_bias = noise(keys[6], (3 * D // 32, 32), 0.5, 3.0, ((0, 2), (1, 16)))
    dense_weight = noise(keys[7], (D, D), (D // 16) ** -0.5, 0.75, ((0, 2), (1, 16)))
    dense_bias = noise(keys[8], (D,), 0.5, 3.0, ((0, 16),))
    expand_weight = noise(keys[9], (D, FF), D ** -0.5, 0.1875, ((0, 16), (1, 2)))
    expand_bias = noise(keys[10], (FF // 32, 32), 0.5, 3.0, ((0, 2), (1, 16)))
    shrink_weight = noise(keys[11], (FF, D), FF ** -0.5, 0.09375, ((0, 2), (1, 16)))
    shrink_bias = noise(keys[12], (D,), 0.5, 3.0, ((0, 16),))
    return {"inputs": inputs, "cotangent": cotangent, "segment_ids": segment_ids, "norm_gain": norm_gain, "norm_shift": norm_shift, "qkv_weight": qkv_weight, "qkv_bias": qkv_bias, "dense_weight": dense_weight, "dense_bias": dense_bias, "expand_weight": expand_weight, "expand_bias": expand_bias, "shrink_weight": shrink_weight, "shrink_bias": shrink_bias}


@jax.custom_vjp
def low(v):
    return lax.optimization_barrier(v.astype(jnp.bfloat16)).astype(jnp.float32)

@jax.custom_vjp
def low_back(v):
    return v

def low_keep(v):
    return (low(v), None)

def low_pass(kept, grad):
    return (grad,)

def back_keep(v):
    return (v, None)

def back_low(kept, grad):
    return (low(grad),)
low.defvjp(low_keep, low_pass)
low_back.defvjp(back_keep, back_low)
epsilon = 1e-05
highest = lax.Precision.HIGHEST

def matmul_high(left, right):
    return jnp.dot(left, right, precision=highest, preferred_element_type=jnp.float32)

def rotary_tables(positions):
    half_rot = ROT // 2
    frequency = 10000.0 ** (-2.0 * jnp.arange(half_rot, dtype=jnp.float32) / ROT)
    angles = positions.astype(jnp.float32)[:, None] * frequency[None, :]
    angles = jnp.concatenate([angles, angles], axis=1)
    return (jnp.cos(angles), jnp.sin(angles))

def rotate(values, cosine, sine):
    head_part = values[..., :ROT]
    first_half = head_part[..., :ROT // 2]
    second_half = head_part[..., ROT // 2:]
    turned = jnp.concatenate([-second_half, first_half], axis=-1)
    rotated = head_part * cosine[:, None, :] + turned * sine[:, None, :]
    return jnp.concatenate([rotated, values[..., ROT:]], axis=-1)

def attend_sequence(operands):
    queries, key_rows, value_rows, segment_row = operands
    positions = jnp.arange(LEN, dtype=jnp.int32)
    allowed = (segment_row[:, None] == segment_row[None, :]) & (positions[:, None] >= positions[None, :])
    scores = low_back(jnp.einsum('qhd,khd->hqk', queries, key_rows, precision=highest))
    scores = jnp.where(allowed[None], scores, -1e+30)
    largest = lax.optimization_barrier(jnp.max(scores, axis=-1, keepdims=True))
    exponent = jnp.exp(scores - largest)
    probs = exponent / lax.optimization_barrier(jnp.sum(exponent, axis=-1, keepdims=True))
    mixture = jnp.einsum('hqk,khd->qhd', low(probs), value_rows, precision=highest)
    return low_back(low(mixture))

def layer_forward(segment_ids, inputs, norm_gain, norm_shift, qkv_weight, qkv_bias, dense_weight, dense_bias, expand_weight, expand_bias, shrink_weight, shrink_bias):
    centered = inputs - lax.optimization_barrier(jnp.mean(inputs, axis=-1, keepdims=True))
    variance = lax.optimization_barrier(jnp.mean(centered * centered, axis=-1, keepdims=True))
    normed = low(centered * lax.rsqrt(variance + epsilon) * norm_gain + norm_shift)
    flat_rows = normed.reshape(SEQS * LEN, D)
    projected = low_back(matmul_high(flat_rows, qkv_weight) + qkv_bias.reshape(3 * D))
    projected = projected.reshape(SEQS, LEN, H, 3 * DH)
    cosine, sine = rotary_tables(jnp.arange(LEN, dtype=jnp.int32))
    queries = low(rotate(projected[..., :DH], cosine, sine) * DH ** (-0.5))
    key_rows = low(rotate(projected[..., DH:2 * DH], cosine, sine))
    value_rows = low(projected[..., 2 * DH:])
    attended = lax.map(jax.checkpoint(attend_sequence), (queries, key_rows, value_rows, segment_ids))
    attended = attended.reshape(SEQS * LEN, D)
    hidden = low_back(matmul_high(flat_rows, expand_weight) + expand_bias.reshape(FF))
    active = low(jax.nn.gelu(hidden, approximate=False))
    result = inputs.reshape(SEQS * LEN, D) + matmul_high(attended, dense_weight) + matmul_high(active, shrink_weight) + dense_bias + shrink_bias
    return result.reshape(SEQS, LEN, D)

def reference(inputs, cotangent, segment_ids, norm_gain, norm_shift, qkv_weight, qkv_bias, dense_weight, dense_bias, expand_weight, expand_bias, shrink_weight, shrink_bias):
    floats = [argument.astype(jnp.float32) for argument in (inputs, norm_gain, norm_shift, qkv_weight, qkv_bias, dense_weight, dense_bias, expand_weight, expand_bias, shrink_weight, shrink_bias)]
    result, pullback = jax.vjp(partial(layer_forward, segment_ids), *floats)
    grads = pullback(cotangent.astype(jnp.float32))
    return (result.astype(jnp.bfloat16), grads[0], grads[1], grads[2], grads[3], grads[4], grads[5], grads[6], grads[7], grads[8], grads[9], grads[10])
```

```python
from functools import partial

import jax
import jax.numpy as jnp
from jax import lax
from jax.experimental import pallas as pl
from jax.experimental.pallas import tpu as pltpu
from jax.sharding import PartitionSpec as P

DH = 64
ROT = 16
PAIR = 2 * DH
EPS = 1e-05
AX = ("fsdp", "ctx")
F32 = jnp.float32
BF16 = jnp.bfloat16


def params(vmem_mib=48):
    return pltpu.CompilerParams(vmem_limit_bytes=vmem_mib << 20)


def nn(a, b):
    return lax.dot_general(a, b, (((1,), (0,)), ((), ())), preferred_element_type=F32)


def nt(a, b):
    return lax.dot_general(a, b, (((1,), (1,)), ((), ())), preferred_element_type=F32)


def tn(a, b):
    return lax.dot_general(a, b, (((0,), (0,)), ((), ())), preferred_element_type=F32)


def sds(shape, dtype):
    return jax.ShapeDtypeStruct(shape, dtype)


def rotary_tables(positions):
    lane = lax.broadcasted_iota(jnp.int32, (positions.shape[0], PAIR), 1) % DH
    half = ROT // 2
    frequency = 10000.0 ** (-2.0 * (lane % half).astype(F32) / ROT)
    angles = positions.astype(F32)[:, None] * frequency
    cosine, sine = jnp.cos(angles), jnp.sin(angles)
    own = jnp.where(lane < ROT, cosine, 1.0)
    ahead = jnp.where(lane < half, -sine, 0.0)
    behind = jnp.where((lane >= half) & (lane < ROT), sine, 0.0)
    return own, ahead, behind


def turn(x, own, ahead, behind, sign):
    half = ROT // 2
    moved = pltpu.roll(x, PAIR - half, 1) * ahead + pltpu.roll(x, half, 1) * behind
    return x * own + moved if sign > 0 else x * own - moved


def prep_cot(cot):
    t, d = cot.shape
    bt = min(256, t)

    def kern(c_ref, ct_ref, sum_ref):
        c = c_ref[...].astype(F32)
        ct_ref[...] = c.T.astype(BF16)

        @pl.when(pl.program_id(0) == 0)
        def _():
            sum_ref[...] = jnp.zeros_like(sum_ref)

        sum_ref[...] += jnp.sum(c, axis=0, keepdims=True)

    return pl.pallas_call(
        kern,
        grid=(t // bt,),
        in_specs=[pl.BlockSpec((bt, d), lambda i: (i, 0))],
        out_specs=[pl.BlockSpec((d, bt), lambda i: (0, i)), pl.BlockSpec((1, d), lambda i: (0, 0))],
        out_shape=[sds((d, t), BF16), sds((1, d), F32)],
        compiler_params=params(),
        name="prep_cot",
    )(cot)


def unit_of(x):
    rows = x.astype(F32)
    centered = rows - jnp.mean(rows, axis=-1, keepdims=True)
    inv = lax.rsqrt(jnp.mean(centered * centered, axis=-1, keepdims=True) + EPS)
    return centered * inv, inv


def layer_norm(x, gain, shift, transposed):
    t, d = x.shape
    bt = min(256, t)

    def kern(x_ref, g_ref, s_ref, n_ref, *rest):
        unit, _ = unit_of(x_ref[...])
        normed = unit * g_ref[...] + s_ref[...]
        n_ref[...] = normed.astype(BF16)
        if transposed:
            rest[0][...] = normed.T.astype(BF16)

    out_specs = [pl.BlockSpec((bt, d), lambda i: (i, 0))]
    out_shape = [sds((t, d), BF16)]
    if transposed:
        out_specs.append(pl.BlockSpec((d, bt), lambda i: (0, i)))
        out_shape.append(sds((d, t), BF16))
    return pl.pallas_call(
        kern,
        grid=(t // bt,),
        in_specs=[
            pl.BlockSpec((bt, d), lambda i: (i, 0)),
            pl.BlockSpec((1, d), lambda i: (0, 0)),
            pl.BlockSpec((1, d), lambda i: (0, 0)),
        ],
        out_specs=out_specs,
        out_shape=out_shape,
        compiler_params=params(),
        name="layer_norm",
    )(x, gain, shift)


def project(lhs, weight, bias, tables, first, count, hw, rotary):
    t, d = lhs.shape
    bt = min(512, t)

    def kern(l_ref, w_ref, b_ref, own_ref, ahead_ref, behind_ref, o_ref):
        part = pl.program_id(0) + first
        acc = nn(l_ref[...], w_ref[...])
        if not rotary:
            o_ref[0] = acc.astype(BF16)
            return
        acc = acc + b_ref[...]

        @pl.when(part < 2)
        def _():
            scale = jnp.where(part == 0, DH**-0.5, 1.0).astype(F32)
            own, ahead, behind = own_ref[...], ahead_ref[...], behind_ref[...]
            for p in range(hw // PAIR):
                cols = slice(p * PAIR, (p + 1) * PAIR)
                o_ref[0, :, cols] = (turn(acc[:, cols], own, ahead, behind, 1) * scale).astype(BF16)

        @pl.when(part >= 2)
        def _():
            o_ref[0] = acc.astype(BF16)

    tab = pl.BlockSpec((bt, PAIR), lambda p, i: (i, 0))
    return pl.pallas_call(
        kern,
        grid=(count, t // bt),
        in_specs=[
            pl.BlockSpec((bt, d), lambda p, i: (i, 0)),
            pl.BlockSpec((d, hw), lambda p, i: (0, p + first)),
            pl.BlockSpec((1, hw), lambda p, i: (0, p + first)),
            tab,
            tab,
            tab,
        ],
        out_specs=pl.BlockSpec((1, bt, hw), lambda p, i: (p, i, 0)),
        out_shape=sds((count, t, hw), BF16),
        compiler_params=params(),
        cost_estimate=pl.CostEstimate(
            flops=2 * count * t * d * hw, bytes_accessed=2 * (count * d * hw + t * d), transcendentals=0
        ),
        name="project",
    )(lhs, weight, bias, *tables)


def attention(lo, starts, qkv, out_grad, kv_far, tables):
    _, t, hw = qkv.shape
    pairs = hw // PAIR
    bq = min(256, t)
    bk = bq
    nq = t // bq

    def kern(lo_ref, st_ref, q_ref, k_ref, v_ref, g_ref, kf_ref, vf_ref, own_ref, ahead_ref, behind_ref,
             att_ref, dq_ref, dk_ref, dv_ref, far_ref, ks, vs, vx, s_scr, d_scr, dk_acc, dv_acc):
        i = pl.program_id(1)
        head_a = lax.broadcasted_iota(jnp.int32, (1, PAIR), 1) < DH

        @pl.when(i == 0)
        def _():
            ks[0:t] = kf_ref[0]
            ks[t:] = k_ref[0]
            for base, ref in ((0, vf_ref), (t, v_ref)):
                v = ref[0]
                one = jnp.ones_like(v)
                vs[base : base + t] = v
                vx[0, base : base + t] = jnp.where(head_a, v, one)
                vx[1, base : base + t] = jnp.where(head_a, one, v)
            dk_acc[...] = jnp.zeros_like(dk_acc)
            dv_acc[...] = jnp.zeros_like(dv_acc)

        q, g = q_ref[0], g_ref[0]
        zero = jnp.zeros_like(q)
        qh = (jnp.where(head_a, q, zero), jnp.where(head_a, zero, q))
        gh = (jnp.where(head_a, g, zero), jnp.where(head_a, zero, g))
        first = lo_ref[i]
        last = (t + (i + 1) * bq) // bk
        start = st_ref[0]
        q_index = t + i * bq + lax.broadcasted_iota(jnp.int32, (1, bq), 1)

        def groups(x):
            return x.reshape(bk // 8, 8, bq)

        def score(kb, best):
            rows = pl.ds(pl.multiple_of(kb * bk, bk), bk)
            k = ks[rows]
            k_index = kb * bk + lax.broadcasted_iota(jnp.int32, (bk, bq), 0)
            ok = (k_index <= q_index) & (k_index >= start)
            out = []
            for h in range(2):
                s = jnp.where(ok, nt(k, qh[h]), -1e30)
                s_scr[h, rows] = s
                out.append(jnp.maximum(best[h], jnp.max(groups(s), axis=0)))
            return tuple(out)

        low = jnp.full((8, bq), -1e30, F32)
        best = lax.fori_loop(first, last, score, (low, low))
        best = [jnp.max(b, axis=0, keepdims=True) for b in best]

        def mix(kb, carry):
            rows = pl.ds(pl.multiple_of(kb * bk, bk), bk)
            v = vs[rows]
            out = []
            for h in range(2):
                total, inner, acc = carry[h]
                p = jnp.exp(s_scr[h, rows] - best[h])
                dp = nt(v, gh[h])
                s_scr[h, rows] = p
                d_scr[h, rows] = dp
                total = total + jnp.sum(groups(p), axis=0)
                inner = inner + jnp.sum(groups(p * dp), axis=0)
                acc = acc + tn(p.astype(BF16), vx[h, rows])
                out.append((total, inner, acc))
            return tuple(out)

        z8, zacc = jnp.zeros((8, bq), F32), jnp.zeros((bq, PAIR), F32)
        got = lax.fori_loop(first, last, mix, ((z8, z8, zacc), (z8, z8, zacc)))
        inv, mean = [], []
        for h in range(2):
            total = jnp.sum(got[h][0], axis=0, keepdims=True)
            inv.append(1.0 / total)
            mean.append(jnp.sum(got[h][1], axis=0, keepdims=True) * inv[h])
        oa, ob = got[0][2], got[1][2]
        mixed = jnp.where(head_a, oa, ob)
        totals = pltpu.roll(jnp.where(head_a, ob, oa), DH, 1)
        att_ref[...] = (mixed / totals).astype(BF16)

        def back(kb, carry):
            rows = pl.ds(pl.multiple_of(kb * bk, bk), bk)
            k = ks[rows]
            out = []
            dk, dv = dk_acc[rows], dv_acc[rows]
            for h in range(2):
                p = s_scr[h, rows] * inv[h]
                ds = (p * (d_scr[h, rows] - mean[h])).astype(BF16)
                dv = dv + nn(p.astype(BF16), gh[h])
                dk = dk + nn(ds, qh[h])
                out.append(carry[h] + tn(ds, k))
            dk_acc[rows] = dk
            dv_acc[rows] = dv
            return tuple(out)

        dqa, dqb = lax.fori_loop(first, last, back, (zacc, zacc))
        dq = jnp.where(head_a, dqa, dqb) * (DH**-0.5)
        dq_ref[...] = turn(dq, own_ref[...], ahead_ref[...], behind_ref[...], -1).astype(BF16)

        @pl.when(i == nq - 1)
        def _():
            far_ref[0, 0] = dk_acc[0:t].astype(BF16)
            far_ref[0, 1] = dv_acc[0:t].astype(BF16)
            dk_ref[...] = dk_acc[t:]
            dv_ref[...] = dv_acc[t:]

    def grouped(part):
        return pl.BlockSpec((1, t, PAIR), lambda p, i, lo: (part, 0, p))

    tab = pl.BlockSpec((bq, PAIR), lambda p, i, lo: (i, 0))
    rowspec = pl.BlockSpec((bq, PAIR), lambda p, i, lo: (i, p))
    whole = pl.BlockSpec((t, PAIR), lambda p, i, lo: (0, p))
    work = t * t * hw * 5 * 2
    return pl.pallas_call(
        kern,
        grid_spec=pltpu.PrefetchScalarGridSpec(
            num_scalar_prefetch=1,
            grid=(pairs, nq),
            in_specs=[
                pl.BlockSpec((1, 1, bq), lambda p, i, lo: (i, 0, 0)),
                pl.BlockSpec((1, bq, PAIR), lambda p, i, lo: (0, i, p)),
                grouped(1),
                grouped(2),
                pl.BlockSpec((1, bq, PAIR), lambda p, i, lo: (0, i, p)),
                grouped(0),
                grouped(1),
                tab,
                tab,
                tab,
            ],
            out_specs=[
                rowspec,
                rowspec,
                whole,
                whole,
                pl.BlockSpec((1, 2, t, PAIR), lambda p, i, lo: (p, 0, 0, 0)),
            ],
            scratch_shapes=[
                pltpu.VMEM((2 * t, PAIR), BF16),
                pltpu.VMEM((2 * t, PAIR), BF16),
                pltpu.VMEM((2, 2 * t, PAIR), BF16),
                pltpu.VMEM((2, 2 * t, bq), F32),
                pltpu.VMEM((2, 2 * t, bq), F32),
                pltpu.VMEM((2 * t, PAIR), F32),
                pltpu.VMEM((2 * t, PAIR), F32),
            ],
        ),
        out_shape=[
            sds((t, hw), BF16),
            sds((t, hw), BF16),
            sds((t, hw), F32),
            sds((t, hw), F32),
            sds((pairs, 2, t, PAIR), BF16),
        ],
        compiler_params=params(),
        cost_estimate=pl.CostEstimate(flops=work, bytes_accessed=t * hw * 30, transcendentals=t * t * hw // DH),
        name="attention",
    )(lo, starts, qkv, qkv, qkv, out_grad, kv_far, kv_far, *tables)


def finish_kv(dk, dv, far, tables):
    t, hw = dk.shape
    pairs = hw // PAIR

    def kern(dk_ref, dv_ref, far_ref, own_ref, ahead_ref, behind_ref, o_ref):
        k = dk_ref[...] + far_ref[0, 0].astype(F32)
        o_ref[0] = turn(k, own_ref[...], ahead_ref[...], behind_ref[...], -1).astype(BF16)
        o_ref[1] = (dv_ref[...] + far_ref[0, 1].astype(F32)).astype(BF16)

    col = pl.BlockSpec((t, PAIR), lambda p: (0, p))
    tab = pl.BlockSpec((t, PAIR), lambda p: (0, 0))
    return pl.pallas_call(
        kern,
        grid=(pairs,),
        in_specs=[col, col, pl.BlockSpec((1, 2, t, PAIR), lambda p: (p, 0, 0, 0)), tab, tab, tab],
        out_specs=pl.BlockSpec((2, t, PAIR), lambda p: (0, 0, p)),
        out_shape=sds((2, t, hw), BF16),
        compiler_params=params(),
        name="finish_kv",
    )(dk, dv, far, *tables)


def feed_forward(normed, cot, x, att, dq, dkv, w_a, w_b, bias, row0, rows, hw, ff):
    d = normed.shape[1]
    bt = min(256, rows)
    bf = min(512, ff)
    base = row0 // bt

    def kern(n_ref, c_ref, x_ref, a_ref, dq_ref, dkv_ref, wa_ref, wb_ref, b_ref,
             act_ref, hg_ref, br_ref, ng_ref, hs_ref, qs_ref, us_ref):
        @pl.when(pl.program_id(0) == 0)
        def _():
            hs_ref[...] = jnp.zeros_like(hs_ref)
            qs_ref[...] = jnp.zeros_like(qs_ref)
            us_ref[...] = jnp.zeros_like(us_ref)

        n, c = n_ref[...], c_ref[...]
        dq = dq_ref[...]
        branch = nt(a_ref[...], wa_ref[:, 3 * hw : 4 * hw])
        grad = nt(dq, wa_ref[:, 0:hw])
        qs_ref[:, 0:hw] += jnp.sum(dq.astype(F32), axis=0, keepdims=True)
        for p in range(2):
            dkv = dkv_ref[p]
            cols = slice((p + 1) * hw, (p + 2) * hw)
            grad = grad + nt(dkv, wa_ref[:, cols])
            qs_ref[:, cols] += jnp.sum(dkv.astype(F32), axis=0, keepdims=True)
        for f in range(ff // bf):
            cols = slice(f * bf, (f + 1) * bf)
            shrink = slice(ff + f * bf, ff + (f + 1) * bf)
            h = nn(n, wb_ref[:, cols]) + b_ref[:, cols]
            cdf = 0.5 * (1.0 + lax.erf(h * (2.0**-0.5)))
            act = (h * cdf).astype(BF16)
            slope = cdf + h * jnp.exp(-0.5 * h * h) * 0.3989422804014327
            hg = (nn(c, wb_ref[:, shrink]) * slope).astype(BF16)
            act_ref[:, cols] = act
            hg_ref[:, cols] = hg
            hs_ref[:, cols] += jnp.sum(hg.astype(F32), axis=0, keepdims=True)
            branch = branch + nt(act, wb_ref[:, shrink])
            grad = grad + nt(hg, wb_ref[:, cols])
        br_ref[...] = branch.astype(BF16)
        ng_ref[...] = grad.astype(BF16)
        unit, _ = unit_of(x_ref[...])
        us_ref[0:1] += jnp.sum(grad * unit, axis=0, keepdims=True)
        us_ref[1:2] += jnp.sum(grad, axis=0, keepdims=True)

    def rowspec(w):
        return pl.BlockSpec((bt, w), lambda i: (i + base, 0))

    def full(shape):
        return pl.BlockSpec(shape, lambda i: (0,) * len(shape))

    def out(w):
        return pl.BlockSpec((bt, w), lambda i: (i, 0))

    return pl.pallas_call(
        kern,
        grid=(rows // bt,),
        in_specs=[
            rowspec(d),
            rowspec(d),
            rowspec(d),
            rowspec(hw),
            rowspec(hw),
            pl.BlockSpec((2, bt, hw), lambda i: (0, i + base, 0)),
            full(w_a.shape),
            full(w_b.shape),
            full(bias.shape),
        ],
        out_specs=[out(ff), out(ff), out(d), out(d), full((1, ff)), full((1, 3 * hw)), full((2, d))],
        out_shape=[
            sds((rows, ff), BF16),
            sds((rows, ff), BF16),
            sds((rows, d), BF16),
            sds((rows, d), BF16),
            sds((1, ff), F32),
            sds((1, 3 * hw), F32),
            sds((2, d), F32),
        ],
        compiler_params=params(56),
        cost_estimate=pl.CostEstimate(
            flops=2 * rows * d * (4 * ff + 4 * hw), bytes_accessed=2 * d * (2 * ff + 4 * hw + rows * 4), transcendentals=rows * ff
        ),
        name="feed_forward",
    )(normed, cot, x, att, dq, dkv, w_a, w_b, bias)


def grad_product(place, lhs_t, rhs, core_of, y_of, add, out_dtype):
    zs, _, _, r, t = lhs_t.shape
    n = rhs[0].shape[1]
    ys = 2 if y_of is None else 1
    bn = min(512, n)
    lens = [piece.shape[0] for piece in rhs]

    def kern(place_ref, l_ref, *refs):
        o_ref = refs[-1]
        left = l_ref[...].reshape(zs * ys * r, t)
        acc = None
        at = 0
        for ref, length in zip(refs, lens):
            part = nn(left[:, at : at + length], ref[...])
            acc = part if acc is None else acc + part
            at += length
        acc = acc.reshape(zs, ys, r, bn)
        for extra in refs[len(lens) : -1]:
            acc = acc + extra[...].astype(F32)
        o_ref[...] = acc.astype(out_dtype)

    in_specs = [pl.BlockSpec((zs, 1, ys, r, t), lambda j, s: (0, core_of(s), 0 if y_of is None else y_of(s), 0, 0))]
    in_specs += [pl.BlockSpec((length, bn), lambda j, s: (0, j)) for length in lens]
    for a in add:
        if a.shape[1] == 2:
            in_specs.append(pl.BlockSpec((zs, 1, r, bn), lambda j, s: (0, y_of(s), 0, j)))
        else:
            in_specs.append(pl.BlockSpec((zs, 1, r, bn), lambda j, s: (0, 0, 0, j)))
    return pl.pallas_call(
        kern,
        grid_spec=pltpu.PrefetchScalarGridSpec(
            num_scalar_prefetch=1,
            grid=(n // bn,),
            in_specs=in_specs,
            out_specs=pl.BlockSpec((zs, ys, r, bn), lambda j, s: (0, 0, 0, j)),
        ),
        out_shape=sds((zs, ys, r, n), out_dtype),
        compiler_params=params(),
        cost_estimate=pl.CostEstimate(
            flops=2 * zs * ys * r * t * n, bytes_accessed=2 * t * n + 2 * zs * ys * r * (t + n), transcendentals=0
        ),
        name="grad_product",
    )(place, lhs_t, *rhs, *add)


def spread(order, total, got):
    zs, _, r, n = total.shape

    def kern(order_ref, t_ref, g_ref, own_ref, out_ref):
        s = t_ref[0, 0] + g_ref[0, 0].astype(F32)

        @pl.when(pl.program_id(0) == 0)
        def _():
            own_ref[...] = s

        out_ref[0] = s.astype(BF16)

    blk = pl.BlockSpec((1, 1, r, n), lambda i, o: (o[i], 0, 0, 0))
    return pl.pallas_call(
        kern,
        grid_spec=pltpu.PrefetchScalarGridSpec(
            num_scalar_prefetch=1,
            grid=(zs,),
            in_specs=[blk, blk],
            out_specs=[
                pl.BlockSpec((r, n), lambda i, o: (0, 0)),
                pl.BlockSpec((1, r, n), lambda i, o: (i, 0, 0)),
            ],
        ),
        out_shape=[sds((r, n), F32), sds((zs, r, n), BF16)],
        compiler_params=params(),
        name="spread",
    )(order, total, got)


def finish_output(x, mine, theirs, bias):
    t, d = x.shape
    bt = min(256, t)

    def kern(x_ref, a_ref, b_ref, bias_ref, o_ref):
        both = a_ref[...].astype(F32) + b_ref[...].astype(F32)
        o_ref[...] = (x_ref[...].astype(F32) + both + bias_ref[...]).astype(BF16)

    row = pl.BlockSpec((bt, d), lambda i: (i, 0))
    return pl.pallas_call(
        kern,
        grid=(t // bt,),
        in_specs=[row, row, row, pl.BlockSpec((1, d), lambda i: (0, 0))],
        out_specs=row,
        out_shape=sds((t, d), BF16),
        compiler_params=params(),
        name="finish_output",
    )(x, mine, theirs, bias)


def finish_input(x, cot, mine, theirs, gain):
    t, d = x.shape
    bt = min(256, t)

    def kern(x_ref, c_ref, a_ref, b_ref, gain_ref, o_ref):
        unit, inv = unit_of(x_ref[...])
        g = (a_ref[...].astype(F32) + b_ref[...].astype(F32)) * gain_ref[...]
        inner = g - jnp.mean(g, axis=-1, keepdims=True) - unit * jnp.mean(g * unit, axis=-1, keepdims=True)
        o_ref[...] = c_ref[...].astype(F32) + inv * inner

    row = pl.BlockSpec((bt, d), lambda i: (i, 0))
    return pl.pallas_call(
        kern,
        grid=(t // bt,),
        in_specs=[row, row, row, row, pl.BlockSpec((1, d), lambda i: (0, 0))],
        out_specs=row,
        out_shape=sds((t, d), F32),
        compiler_params=params(),
        name="finish_input",
    )(x, cot, mine, theirs, gain)


def body(
    inputs,
    cotangent,
    segment_ids,
    norm_gain,
    norm_shift,
    qkv_weight,
    qkv_bias,
    dense_weight,
    dense_bias,
    expand_weight,
    expand_bias,
    shrink_weight,
    shrink_bias,
):
    seqs, t, d = inputs.shape
    fsdp, ctx, tp = lax.axis_size("fsdp"), lax.axis_size("ctx"), lax.axis_size("tp")
    assert seqs == 1 and ctx == 2
    zs, n = fsdp // 2, fsdp * ctx
    r = d // n
    hw = dense_weight.shape[0]
    heads = hw // DH
    ff = expand_weight.shape[1]
    f_idx, y_idx, x_idx = lax.axis_index("fsdp"), lax.axis_index("ctx"), lax.axis_index("tp")
    z_idx, core_idx = f_idx // 2, f_idx % 2
    place = jnp.stack([core_idx, y_idx]).astype(jnp.int32)
    z_order = (z_idx ^ jnp.arange(zs, dtype=jnp.int32)).astype(jnp.int32)

    core_pairs = [(i, i ^ 1) for i in range(fsdp)]
    y_pairs = [(0, 1), (1, 0)]

    def z_pairs(s):
        return [(i, (((i // 2) ^ s) * 2) + i % 2) for i in range(fsdp)]

    def to_core(a):
        return lax.ppermute(a, "fsdp", core_pairs)

    def to_y(a):
        return lax.ppermute(a, "ctx", y_pairs)

    def to_z(a, s):
        return lax.ppermute(a, "fsdp", z_pairs(s))

    def tp_terms(a):
        if tp == 2:
            return a, lax.ppermute(a, "tp", [(0, 1), (1, 0)])
        return lax.psum(a.astype(F32), "tp"), jnp.zeros_like(a)

    x, cot = inputs[0], cotangent[0]

    if tp == 2:
        piece = lax.dynamic_slice_in_dim(x, x_idx * (t // 2), t // 2, 0)
        near = lax.ppermute(piece, "ctx", [(0, 1)])
        across = lax.ppermute(near, "tp", [(0, 1), (1, 0)])
        x_far = jnp.where(x_idx == 0, jnp.concatenate([near, across]), jnp.concatenate([across, near]))
    else:
        x_far = lax.ppermute(x, "ctx", [(0, 1)])

    w_a = jnp.concatenate(
        [qkv_weight.reshape(r, heads, 3, DH).transpose(0, 2, 1, 3).reshape(r, 3 * hw), dense_weight.T], axis=1
    )
    w_b = jnp.concatenate([expand_weight, shrink_weight.T], axis=1)
    small = jnp.concatenate(
        [norm_gain, norm_shift, dense_bias, shrink_bias, qkv_bias.reshape(-1), expand_bias.reshape(-1)]
    )[None]
    small = lax.all_gather(small, AX, axis=0, tiled=True)
    w_a = lax.all_gather(w_a, AX, axis=0, tiled=True)
    w_b = lax.all_gather(w_b, AX, axis=0, tiled=True)

    def vec(k):
        return small[:, k * r : (k + 1) * r].astype(F32).reshape(1, d)

    gain, shift, bias_total = vec(0), vec(1), vec(2) + vec(3)
    q_rows, q_cols = qkv_bias.shape
    e_rows, e_cols = expand_bias.shape
    q_bias = small[:, 4 * r : 4 * r + q_rows * q_cols].astype(F32).reshape(n, q_rows, q_cols)
    q_bias = q_bias.transpose(1, 0, 2).reshape(heads, 3, DH).transpose(1, 0, 2).reshape(1, 3 * hw)
    q_bias = jnp.concatenate([q_bias, jnp.zeros((1, hw), F32)], axis=1)
    e_bias = small[:, 4 * r + q_rows * q_cols :].astype(F32).reshape(n, e_rows, e_cols)
    e_bias = e_bias.transpose(1, 0, 2).reshape(1, ff)

    start_row = y_idx * t
    seg = segment_ids[0]
    seg_here = lax.dynamic_slice_in_dim(seg, start_row, t, 0)
    starts = jnp.sum((seg[:, None] < seg_here[None, :]).astype(jnp.int32), axis=0) - start_row + t
    bq = min(256, t)
    nq = t // bq
    starts = starts.reshape(nq, 1, bq)
    lo = starts[:, 0, 0] // bq
    positions = start_row + jnp.arange(t, dtype=jnp.int32)
    tables = rotary_tables(positions)
    far_tables = rotary_tables(positions - t)

    cot_t, cot_sum = prep_cot(cot)
    normed, normed_t = layer_norm(x, gain, shift, True)
    (normed_far,) = layer_norm(x_far, gain, shift, False)
    cot_t = cot_t.reshape(zs, 2, 2, r, t)
    normed_t = normed_t.reshape(zs, 2, 2, r, t)

    out_grad = project(cot, w_a, q_bias, tables, 3, 1, hw, False)
    qkv = project(normed, w_a, q_bias, tables, 0, 3, hw, True)
    kv_far = project(normed_far, w_a, q_bias, far_tables, 1, 2, hw, True)
    att, dq, dk, dv, far = attention(lo, starts, qkv, out_grad, kv_far, tables)
    far = lax.ppermute(far, "ctx", [(1, 0)])
    dkv = finish_kv(dk, dv, far, tables)

    own = lambda s: s[0]
    partner = lambda s: 1 - s[0]
    here = lambda s: s[1]
    there = lambda s: 1 - s[1]

    def reduce_grad(lhs_t, rhs):
        given = grad_product(place, lhs_t, rhs, partner, None, [], BF16)
        from_core = to_core(given)
        given = grad_product(place, lhs_t, rhs, own, there, [from_core], BF16)
        from_y = to_y(given)
        total = grad_product(place, lhs_t, rhs, own, here, [from_core], F32)
        total, pieces = spread(z_order, total, from_y)
        for s in range(1, zs):
            total = total + to_z(pieces[s], s).astype(F32)
        return total

    dense_grad = reduce_grad(cot_t, [att])
    pg_grads = [reduce_grad(normed_t, [dq]), reduce_grad(normed_t, [dkv[0]]), reduce_grad(normed_t, [dkv[1]])]

    chunks = 2
    rows = t // chunks
    outs = [
        feed_forward(normed, cot, x, att, dq, dkv, w_a, w_b, e_bias, c * rows, rows, hw, ff) for c in range(chunks)
    ]
    act, hg, br, ng, h_sum, q_sum, u_sum = [list(o) for o in zip(*outs)]
    br, br_other = zip(*[tp_terms(b) for b in br])
    ng, ng_other = zip(*[tp_terms(g) for g in ng])

    shrink_grad = reduce_grad(cot_t, act)
    expand_grad = reduce_grad(normed_t, hg)

    sums = jnp.concatenate([cot_sum, sum(h_sum), sum(q_sum), sum(u_sum).reshape(1, 2 * d)], axis=1)
    sums = sums + to_core(sums)
    sums = sums + to_y(sums)
    sums = sum([to_z(sums, s) for s in range(1, zs)], sums)
    norm_sums = sums[:, d + ff + 3 * hw :]
    if tp == 2:
        norm_sums = norm_sums + lax.ppermute(norm_sums, "tp", [(0, 1), (1, 0)])
    else:
        norm_sums = lax.psum(norm_sums, "tp")
    shard = f_idx * ctx + y_idx

    def own_vec(v):
        return lax.dynamic_index_in_dim(v.reshape(n, r), shard, 0, keepdims=False)

    bias_grad = own_vec(sums[:, :d])
    expand_bias_grad = sums[:, d : d + ff].reshape(e_rows, n, e_cols)
    expand_bias_grad = lax.dynamic_index_in_dim(expand_bias_grad, shard, 1, keepdims=False)
    qkv_bias_grad = sums[:, d + ff : d + ff + 3 * hw].reshape(3, heads, DH).transpose(1, 0, 2)
    qkv_bias_grad = qkv_bias_grad.reshape(q_rows, n, q_cols)
    qkv_bias_grad = lax.dynamic_index_in_dim(qkv_bias_grad, shard, 1, keepdims=False)

    layer_output = finish_output(x, jnp.concatenate(br), jnp.concatenate(br_other), bias_total)
    input_grad = finish_input(x, cot, jnp.concatenate(ng), jnp.concatenate(ng_other), gain)
    qkv_grad = jnp.concatenate(pg_grads, axis=1).reshape(r, 3, heads, DH).transpose(0, 2, 1, 3).reshape(r, 3 * hw)
    return (
        layer_output[None],
        input_grad[None],
        own_vec(norm_sums[:, :d]),
        own_vec(norm_sums[:, d:]),
        qkv_grad,
        qkv_bias_grad,
        dense_grad.T,
        bias_grad,
        expand_grad,
        expand_bias_grad,
        shrink_grad.T,
        bias_grad,
    )


def solution(mesh):
    both = ("fsdp", "ctx")
    in_specs = (
        P("fsdp", "ctx", None),
        P("fsdp", "ctx", None),
        P("fsdp", None),
        P(both),
        P(both),
        P(both, "tp"),
        P("tp", both),
        P("tp", both),
        P(both),
        P(both, "tp"),
        P("tp", both),
        P("tp", both),
        P(both),
    )
    out_specs = (
        P("fsdp", "ctx", None),
        P("fsdp", "ctx", None),
        P(both),
        P(both),
        P(both, "tp"),
        P("tp", both),
        P("tp", both),
        P(both),
        P(both, "tp"),
        P("tp", both),
        P("tp", both),
        P(both),
    )
    return jax.shard_map(body, mesh=mesh, in_specs=in_specs, out_specs=out_specs, check_vma=False)
```
